32 devices in a mesh: tm: 4 (over z), space: 8 (over y, x, core).
Axes of the slice: x: 2, y: 2, z: 4, core: 2. Of those that a mesh axis runs over, the one named last changes fastest.
Arguments:
- positions: float32 [3, 8192], P(None, 'space'), may hold values from -6 to 6
- strengths: float32 [3, 8192], P(None, 'space'), may hold values from -6 to 6
- source_lists: int32 [64, 8], P('space'), may hold values from 0 to 63, as said below
- block_slot: int32 [64], replicated, may hold values from 0 to 63, as said below
Outputs:
- slice_ends: float32 [4, 6, 8192], P('tm', None, 'space')
The draws below stay inside these ranges and needn't reach their ends.
Inputs may be any that keep to these rules, and one draw needn't show every extreme that they name: `source_lists`: the 8 ids of a row are distinct. Logical block g is stored as block block_slot[g], on space device block_slot[g] // 8. Among all entries of the 8 rows of one space device, at most 16 are stored on any one space device, and one space device, the same for all rows, holds exactly 16 of the entries of every space device. `block_slot`: A permutation of the logical block ids.
All inputs are finite; a program needn't handle non-finite values.
Results may differ from the reference program's by a relative error of at most 0.0003.
Values sent between devices are 32-bit elements; how exact they have to be, the bound alone decides.
A program may use at most 64 MiB of HBM per device.

```python
import jax
import jax.numpy as jnp
from jax import lax

BLOCK = 128
BLK_DEV = 8
LIST = 8
ITERS = 2
SLICES = 4
NB = 64
NP = 8192
CAP = 16
N_SPACE = 8


def joint_tables(key):
    base_key = jax.random.fold_in(key, 7013)
    slot_key, hot_key, rest_key = jax.random.split(base_key, 3)
    block_slot = jax.random.permutation(slot_key, NB).astype(jnp.int32)
    logical_of = jnp.argsort(block_slot).astype(jnp.int32)
    hot_owner = jax.random.randint(hot_key, (), 0, N_SPACE).astype(jnp.int32)
    request_count = BLK_DEV * LIST
    owner_pool = jnp.repeat(jnp.arange(N_SPACE, dtype=jnp.int32), CAP)

    def one_device(device_key):
        pick_key, local_key, order_key = jax.random.split(device_key, 3)
        scores = jax.random.permutation(pick_key, N_SPACE * CAP).astype(jnp.int32)
        scores = jnp.where(owner_pool == hot_owner, scores - N_SPACE * CAP, scores)
        chosen = owner_pool[jnp.argsort(scores)[:request_count]]
        owners = jnp.sort(chosen)
        onehot = (owners[:, None] == jnp.arange(N_SPACE, dtype=jnp.int32)[None, :]).astype(jnp.int32)
        counts = jnp.sum(onehot, 0)
        group_starts = jnp.cumsum(counts) - counts
        first_of = jnp.sum(onehot * group_starts[None, :], 1)
        serial = jnp.arange(request_count, dtype=jnp.int32)
        rank_within = (serial - first_of) // BLK_DEV
        list_of = serial % BLK_DEV
        local_perm = jnp.argsort(jax.random.randint(local_key, (BLK_DEV, N_SPACE, BLK_DEV), 0, 2 ** 30), axis=-1).astype(jnp.int32)
        local_index = local_perm[list_of, owners, rank_within]
        logical = logical_of[owners * BLK_DEV + local_index]
        table = logical.reshape(LIST, BLK_DEV).T
        shuffle = jnp.argsort(jax.random.randint(order_key, (BLK_DEV, LIST), 0, 2 ** 30), axis=1)
        return jnp.take_along_axis(table, shuffle, axis=1).astype(jnp.int32)
    device_keys = jax.random.split(rest_key, N_SPACE)
    tables = jax.vmap(one_device)(device_keys)
    return (tables.reshape(NB, LIST).astype(jnp.int32), block_slot)


def draw_source_lists(key, part):
    return joint_tables(key)[0]


def draw_block_slot(key, part):
    return joint_tables(key)[1]


def block_levels(key, extent, shards, low, high):
    gain = 1.0
    for axis_at, shards_of in shards:
        heights = jax.random.uniform(jax.random.fold_in(jax.random.fold_in(key, 6), axis_at), (shards_of,), jnp.float32, low / len(shards), high / len(shards))
        gain = gain * jnp.repeat(jnp.exp(heights), extent[axis_at] // shards_of).reshape((-1,) + (1,) * (len(extent) - 1 - axis_at))
    return gain


def bell_draw(rng, extent, width, most, pieces=(), kind=jnp.bfloat16):
    drawn = width * jax.random.normal(rng, extent, jnp.float32)
    if pieces:
        drawn = drawn * block_levels(rng, extent, pieces, -0.22, 0.18)
    return jnp.clip(drawn, -most, most).astype(kind)


def setup_inputs(seed: int = 0) -> dict:
    keys = jax.random.split(jax.random.key(seed), 5)
    return {
        "positions": bell_draw(keys[0], (3, NP), 1.0, 6.0, ((1, 8),), jnp.float32),
        "strengths": bell_draw(keys[1], (3, NP), 1.0, 6.0, ((1, 8),), jnp.float32),
        "source_lists": draw_source_lists(jax.random.fold_in(keys[4], 71), 0),
        "block_slot": draw_block_slot(jax.random.fold_in(keys[4], 71), 0),
    }


time_step = 0.1
core_square = 0.25
inv_four_pi = 0.07957747154594767

def cross_product(first_vec, second_vec):
    return jnp.stack([first_vec[1] * second_vec[2] - first_vec[2] * second_vec[1], first_vec[2] * second_vec[0] - first_vec[0] * second_vec[2], first_vec[0] * second_vec[1] - first_vec[1] * second_vec[0]], 0)

def interact(target, source):
    separation = target[0:3, None, :] - source[0:3, :, None]
    rho_squared = lax.optimization_barrier(jnp.sum(separation * separation, 0)) + core_square
    inverse = lax.rsqrt(rho_squared)
    kernel_three = inverse * inverse * inverse
    kernel_five = kernel_three * inverse * inverse
    alpha_source = source[3:6, :, None]
    alpha_target = target[3:6, None, :]
    r_cross = cross_product(separation, alpha_source)
    a_cross = cross_product(alpha_target, alpha_source)
    a_dot_r = lax.optimization_barrier(jnp.sum(alpha_target * separation, 0))
    velocity = -inv_four_pi * lax.optimization_barrier(jnp.sum(kernel_three * r_cross, 1))
    stretch = -inv_four_pi * lax.optimization_barrier(jnp.sum(kernel_three * a_cross - 3.0 * kernel_five * a_dot_r * r_cross, 1))
    return jnp.concatenate([velocity, stretch], 0)

def evaluate(state_now, source_lists, block_slot):
    tiled_state = state_now.reshape(6, -1, BLOCK)

    def one_block(block_index):
        physical = block_slot[source_lists[block_index]]
        source = tiled_state[:, physical].reshape(6, -1)
        target = lax.dynamic_index_in_dim(tiled_state, block_index, 1, keepdims=False)
        return interact(target, source)
    rate_blocks = lax.map(one_block, jnp.arange(tiled_state.shape[1], dtype=jnp.int32))
    return jnp.moveaxis(rate_blocks, 0, 1).reshape(6, -1)

def fine_sweep(start_state, rate_zero, source_lists, block_slot):
    half_step = 0.5 * time_step
    node_one = start_state + half_step * rate_zero
    rate_one = evaluate(node_one, source_lists, block_slot)
    node_two = node_one + half_step * rate_one
    rate_two = evaluate(node_two, source_lists, block_slot)
    second_one = start_state + time_step * (5.0 / 24.0 * rate_zero + 1.0 / 3.0 * rate_one - 1.0 / 24.0 * rate_two)
    second_rate = evaluate(second_one, source_lists, block_slot)
    return second_one + half_step * (second_rate - rate_one) + time_step * (-1.0 / 24.0 * rate_zero + 1.0 / 3.0 * rate_one + 5.0 / 24.0 * rate_two)

def reference(positions, strengths, source_lists, block_slot):
    initial = jnp.concatenate([positions, strengths], 0)
    rate_initial = evaluate(initial, source_lists, block_slot)
    start_list = [initial] * SLICES
    rate_list = [rate_initial] * SLICES
    end_list = []
    for iteration in range(ITERS):
        corrections = []
        for slice_index in range(SLICES):
            fine_end = fine_sweep(start_list[slice_index], rate_list[slice_index], source_lists, block_slot)
            corrections.append(fine_end - (start_list[slice_index] + time_step * rate_list[slice_index]))
        current = initial
        new_starts = []
        new_rates = []
        end_list = []
        for slice_index in range(SLICES):
            rate_now = evaluate(current, source_lists, block_slot)
            new_starts.append(current)
            new_rates.append(rate_now)
            end_state = current + time_step * rate_now + corrections[slice_index]
            end_list.append(end_state)
            current = end_state
        start_list = new_starts
        rate_list = new_rates
    return jnp.stack(end_list, 0)
```

```python
import functools

import jax
import jax.numpy as jnp
from jax import lax
from jax.experimental import pallas as pl
from jax.experimental.pallas import tpu as pltpu
from jax.sharding import PartitionSpec as P

BLOCK = 128
SUB = 8
PIECES = 6
MESH = pl.DeviceIdType.MESH

time_step = 0.1
core_square = 0.25
inv_four_pi = 0.07957747154594767


def cross(u, v):
    return [
        u[1] * v[2] - u[2] * v[1],
        u[2] * v[0] - u[0] * v[2],
        u[0] * v[1] - u[1] * v[0],
    ]


def dot3(u, v):
    return u[0] * v[0] + u[1] * v[1] + u[2] * v[2]


def rounded(v):
    return v.astype(jnp.bfloat16).astype(jnp.float32)


def split3(v):
    high = rounded(v)
    rest = v - high
    middle = rounded(rest)
    return high, middle, rounded(rest - middle)


def kernel(
    spaces, slices, blocks, width,
    pos_ref, str_ref, list_ref, slot_ref, out_ref,
    gathered, base, rate, f0, f1, f2, c0, incoming, outgoing,
    rows_a, rows_b, feat, moment, coef, send_sem, recv_sem, pass_sem,
):
    me = lax.axis_index("space")
    g = lax.axis_index("tm")
    h = time_step

    barrier = pltpu.get_barrier_semaphore()

    def greet(d, carry):
        peer = lax.rem(me + d, spaces)
        pl.semaphore_signal(barrier, inc=1, device_id={"space": peer}, device_id_type=MESH)
        return carry

    lax.fori_loop(1, spaces, greet, 0)

    @pl.when(g > 0)
    def _():
        pl.semaphore_signal(barrier, inc=1, device_id={"tm": g - 1}, device_id_type=MESH)

    @pl.when(g < slices - 1)
    def _():
        pl.semaphore_signal(barrier, inc=1, device_id={"tm": g + 1}, device_id_type=MESH)

    for b in range(blocks):
        cols = slice(b * BLOCK, (b + 1) * BLOCK)
        for r in range(3):
            gathered[0, me, r, b : b + 1, :] = pos_ref[r : r + 1, cols]
            gathered[0, me, 3 + r, b : b + 1, :] = str_ref[r : r + 1, cols]

    neighbours = jnp.where(g > 0, 1, 0) + jnp.where(g < slices - 1, 1, 0)
    pl.semaphore_wait(barrier, spaces - 1 + neighbours)

    def copy_to(slot, d):
        peer = lax.rem(me + d, spaces)
        return pltpu.make_async_remote_copy(
            src_ref=gathered.at[slot, me],
            dst_ref=gathered.at[slot, me],
            send_sem=send_sem.at[slot, d],
            recv_sem=recv_sem.at[slot, d],
            device_id={"space": peer},
            device_id_type=MESH,
        )

    def copy_from(slot, d):
        peer = lax.rem(me + spaces - d, spaces)
        return peer, pltpu.make_async_remote_copy(
            src_ref=gathered.at[slot, me],
            dst_ref=gathered.at[slot, peer],
            send_sem=send_sem.at[slot, d],
            recv_sem=recv_sem.at[slot, d],
            device_id={"space": peer},
            device_id_type=MESH,
        )

    def pass_copy():
        return pltpu.make_async_remote_copy(
            src_ref=outgoing,
            dst_ref=incoming,
            send_sem=pass_sem.at[0],
            recv_sem=pass_sem.at[1],
            device_id={"tm": lax.rem(g + 1, slices)},
            device_id_type=MESH,
        )

    def rows_of(ref, values):
        for r, v in enumerate(values):
            ref[pl.ds(r, blocks, stride=SUB), :] = v

    def source_features(slot, p):
        x = [gathered[slot, p, r] for r in range(3)]
        a = [gathered[slot, p, 3 + r] for r in range(3)]
        zero = jnp.zeros_like(x[0])
        rows_of(rows_a, x + a + [dot3(x, x), zero + 1.0])
        rows_of(rows_b, a + cross(x, a) + [zero, zero])
        high, middle, low = split3(rows_a[...].reshape(blocks, SUB, BLOCK))
        feat[pl.ds(p * blocks, blocks)] = jnp.concatenate(
            [high, high, high, middle, middle, low], 1
        ).astype(jnp.bfloat16)
        whole = rows_b[...].reshape(blocks, SUB, BLOCK)
        high = rounded(whole)
        moment[pl.ds(p * blocks, blocks)] = jnp.concatenate(
            [high, whole - high], 1
        ).astype(jnp.bfloat16)

    def target_features(slot):
        x = [gathered[slot, me, r] for r in range(3)]
        a = [gathered[slot, me, 3 + r] for r in range(3)]
        zero = jnp.zeros_like(x[0])
        rows_of(rows_a, [-2.0 * v for v in x] + [zero] * 3 + [zero + 1.0, dot3(x, x) + core_square])
        rows_of(rows_b, [-v for v in a] + [zero] * 4 + [dot3(a, x)])
        for half, ref in enumerate((rows_a, rows_b)):
            high, middle, low = split3(ref[...].reshape(blocks, SUB, BLOCK))
            coef[:, :, half * BLOCK : (half + 1) * BLOCK] = jnp.concatenate(
                [high, middle, low, high, middle, high], 1
            ).astype(jnp.bfloat16)

    def one_target(i, carry):
        left = coef[i]
        total = jnp.zeros((2 * SUB, 2 * BLOCK), jnp.float32)
        group = 2 if width % 2 == 0 else 1
        for j in range(0, width, group):
            at = [slot_ref[list_ref[i, j + k]] for k in range(group)]
            right = jnp.concatenate([feat[p] for p in at], 1)
            both = lax.dot_general(
                left, right, (((0,), (0,)), ((), ())), preferred_element_type=jnp.float32
            )
            inverse = lax.rsqrt(both[:BLOCK])
            square = inverse * inverse
            three = square * inverse
            five = three * (square * both[BLOCK:])
            weight = jnp.concatenate([three, five], 0)
            high = weight.astype(jnp.bfloat16)
            low = (weight - high.astype(jnp.float32)).astype(jnp.bfloat16)
            sums = jnp.concatenate([moment[p] for p in at], 1)
            for part in (high, low):
                total += lax.dot_general(
                    sums, part, (((1,), (1,)), ((), ())), preferred_element_type=jnp.float32
                )
        whole = total[:SUB] + total[SUB:]
        at_rows = pl.ds(pl.multiple_of(i * SUB, SUB), SUB)
        rows_a[at_rows, :] = whole[:, :BLOCK]
        rows_b[at_rows, :] = whole[:, BLOCK:]
        return carry

    def evaluate(slot):
        for d in range(1, spaces):
            copy_to(slot, d).start()
        target_features(slot)
        source_features(slot, me)

        def arrive(d, carry):
            peer, copy = copy_from(slot, d)
            copy.wait_recv()
            source_features(slot, peer)
            return carry

        lax.fori_loop(1, spaces, arrive, 0)
        lax.fori_loop(0, blocks, one_target, 0)
        x = [gathered[slot, me, r] for r in range(3)]
        a = [gathered[slot, me, 3 + r] for r in range(3)]
        pick = lambda ref, r: ref[pl.ds(r, blocks, stride=SUB), :]
        three_a = [pick(rows_a, r) for r in range(3)]
        three_b = [pick(rows_a, 3 + r) for r in range(3)]
        five_a = [pick(rows_b, r) for r in range(3)]
        five_b = [pick(rows_b, 3 + r) for r in range(3)]
        cross_v = cross(x, three_a)
        cross_s = cross(a, three_a)
        cross_f = cross(x, five_a)
        for r in range(3):
            rate[r] = -inv_four_pi * (cross_v[r] - three_b[r])
            rate[3 + r] = -inv_four_pi * (cross_s[r] - 3.0 * (cross_f[r] - five_b[r]))
        for d in range(1, spaces):
            copy_to(slot, d).wait_send()

    def write_out(value):
        for b in range(blocks):
            for r in range(6):
                out_ref[0, r : r + 1, b * BLOCK : (b + 1) * BLOCK] = value[r, b : b + 1, :]

    second = 3 + g
    steps = jnp.where(g == 0, 4, jnp.where(g < slices - 1, g + 8, g + 7))

    def step(s, carry):
        slot = lax.rem(s, 2)
        other = 1 - slot
        evaluate(slot)
        current = gathered[slot, me]
        now = rate[...]
        part = jnp.where(s < 4, s, s - second)

        @pl.when(part == 0)
        def _():
            base[...] = current
            f0[...] = now
            gathered[other, me] = current + (0.5 * h) * now

        @pl.when(part == 1)
        def _():
            f1[...] = now
            gathered[other, me] = current + (0.5 * h) * now

        @pl.when(part == 2)
        def _():
            f2[...] = now
            gathered[other, me] = base[...] + h * (
                5.0 / 24.0 * f0[...] + 1.0 / 3.0 * f1[...] - 1.0 / 24.0 * now
            )

        @pl.when(part == 3)
        def _():
            end = (
                current
                + (0.5 * h) * (now - f1[...])
                + h * (-1.0 / 24.0 * f0[...] + 1.0 / 3.0 * f1[...] + 5.0 / 24.0 * f2[...])
            )
            coarse = base[...] + h * f0[...]
            correction = end - coarse

            @pl.when(s == 3)
            def _():
                c0[...] = correction

            @pl.when((s > 3) & (g > 1))
            def _():
                pass_copy().wait_recv()
                gathered[other, me] = incoming[...] + correction

            @pl.when((s == 3) | (g <= 1))
            def _():
                gathered[other, me] = coarse + correction

            @pl.when((s > 3) | (g == 0))
            def _():
                write_out(gathered[other, me])

        @pl.when(part < 0)
        def _():
            gathered[other, me] = current + h * now + c0[...]

        @pl.when(part == 4)
        def _():
            outgoing[...] = current + h * now
            copy = pass_copy()
            copy.start()
            copy.wait_send()

        return carry

    lax.fori_loop(0, steps, step, 0)


def per_device(spaces, slices, positions, strengths, source_lists, block_slot):
    blocks, width = source_lists.shape
    whole = block_slot.shape[0]
    state = pltpu.VMEM((6, blocks, BLOCK), jnp.float32)
    vmem = pl.BlockSpec(memory_space=pltpu.VMEM)
    smem = pl.BlockSpec(memory_space=pltpu.SMEM)
    return pl.pallas_call(
        functools.partial(kernel, spaces, slices, blocks, width),
        out_shape=jax.ShapeDtypeStruct((1, 6, blocks * BLOCK), jnp.float32),
        in_specs=[vmem, vmem, smem, smem],
        out_specs=vmem,
        scratch_shapes=[
            pltpu.VMEM((2, spaces, 6, blocks, BLOCK), jnp.float32),
            state, state, state, state, state, state, state, state,
            pltpu.VMEM((blocks * SUB, BLOCK), jnp.float32),
            pltpu.VMEM((blocks * SUB, BLOCK), jnp.float32),
            pltpu.VMEM((whole, PIECES * SUB, BLOCK), jnp.bfloat16),
            pltpu.VMEM((whole, 2 * SUB, BLOCK), jnp.bfloat16),
            pltpu.VMEM((blocks, PIECES * SUB, 2 * BLOCK), jnp.bfloat16),
            pltpu.SemaphoreType.DMA((2, spaces)),
            pltpu.SemaphoreType.DMA((2, spaces)),
            pltpu.SemaphoreType.DMA((2,)),
        ],
        compiler_params=pltpu.CompilerParams(collective_id=0, has_side_effects=True),
    )(positions, strengths, source_lists, block_slot)


def solution(mesh):
    return jax.shard_map(
        functools.partial(per_device, mesh.shape["space"], mesh.shape["tm"]),
        mesh=mesh,
        in_specs=(P(None, "space"), P(None, "space"), P("space", None), P()),
        out_specs=P("tm", None, "space"),
        check_vma=False,
    )
```

```python
import functools

import jax
import jax.numpy as jnp
from jax import lax
from jax.experimental import pallas as pl
from jax.experimental.pallas import tpu as pltpu
from jax.sharding import PartitionSpec as P

BLOCK = 128
SUB = 8
PIECES = 6
TOGETHER = 8
AHEAD = 2
MESH = pl.DeviceIdType.MESH

time_step = 0.1
core_square = 0.25
inv_four_pi = 0.07957747154594767


def cross(u, v):
    return [
        u[1] * v[2] - u[2] * v[1],
        u[2] * v[0] - u[0] * v[2],
        u[0] * v[1] - u[1] * v[0],
    ]


def dot3(u, v):
    return u[0] * v[0] + u[1] * v[1] + u[2] * v[2]


def rounded(v):
    return v.astype(jnp.bfloat16).astype(jnp.float32)


def split3(v):
    high = rounded(v)
    rest = v - high
    middle = rounded(rest)
    return high, middle, rounded(rest - middle)


def kernel(
    spaces, slices, blocks, width,
    pos_ref, str_ref, list_ref, slot_ref, out_ref,
    gathered, base, rate, f0, f1, f2, c0, incoming, outgoing,
    rows_a, rows_b, feat, moment, coef, send_sem, recv_sem, pass_sem,
):
    me = lax.axis_index("space")
    g = lax.axis_index("tm")
    h = time_step

    barrier = pltpu.get_barrier_semaphore()

    def greet(d, carry):
        peer = lax.rem(me + d, spaces)
        pl.semaphore_signal(barrier, inc=1, device_id={"space": peer}, device_id_type=MESH)
        return carry

    lax.fori_loop(1, spaces, greet, 0)

    @pl.when(g > 0)
    def _():
        pl.semaphore_signal(barrier, inc=1, device_id={"tm": g - 1}, device_id_type=MESH)

    @pl.when(g < slices - 1)
    def _():
        pl.semaphore_signal(barrier, inc=1, device_id={"tm": g + 1}, device_id_type=MESH)

    for b in range(blocks):
        cols = slice(b * BLOCK, (b + 1) * BLOCK)
        for r in range(3):
            gathered[0, me, r, b : b + 1, :] = pos_ref[r : r + 1, cols]
            gathered[0, me, 3 + r, b : b + 1, :] = str_ref[r : r + 1, cols]

    neighbours = jnp.where(g > 0, 1, 0) + jnp.where(g < slices - 1, 1, 0)
    pl.semaphore_wait(barrier, spaces - 1 + neighbours)

    def copy_to(slot, d):
        peer = lax.rem(me + d, spaces)
        return pltpu.make_async_remote_copy(
            src_ref=gathered.at[slot, me],
            dst_ref=gathered.at[slot, me],
            send_sem=send_sem.at[slot, d],
            recv_sem=recv_sem.at[slot, d],
            device_id={"space": peer},
            device_id_type=MESH,
        )

    def copy_from(slot, d):
        peer = lax.rem(me + spaces - d, spaces)
        return peer, pltpu.make_async_remote_copy(
            src_ref=gathered.at[slot, me],
            dst_ref=gathered.at[slot, peer],
            send_sem=send_sem.at[slot, d],
            recv_sem=recv_sem.at[slot, d],
            device_id={"space": peer},
            device_id_type=MESH,
        )

    def pass_copy():
        return pltpu.make_async_remote_copy(
            src_ref=outgoing,
            dst_ref=incoming,
            send_sem=pass_sem.at[0],
            recv_sem=pass_sem.at[1],
            device_id={"tm": lax.rem(g + 1, slices)},
            device_id_type=MESH,
        )

    def rows_of(ref, values):
        for r, v in enumerate(values):
            ref[pl.ds(r, blocks, stride=SUB), :] = v

    def source_features(slot, p):
        x = [gathered[slot, p, r] for r in range(3)]
        a = [gathered[slot, p, 3 + r] for r in range(3)]
        zero = jnp.zeros_like(x[0])
        rows_of(rows_a, x + a + [dot3(x, x), zero + 1.0])
        rows_of(rows_b, a + cross(x, a) + [zero, zero])
        high, middle, low = split3(rows_a[...].reshape(blocks, SUB, BLOCK))
        feat[pl.ds(p * blocks, blocks)] = jnp.concatenate(
            [high, high, high, middle, middle, low], 1
        ).astype(jnp.bfloat16)
        whole = rows_b[...].reshape(blocks, SUB, BLOCK)
        high = rounded(whole)
        moment[pl.ds(p * blocks, blocks)] = jnp.concatenate(
            [high, whole - high], 1
        ).astype(jnp.bfloat16)

    def target_features(slot):
        x = [gathered[slot, me, r] for r in range(3)]
        a = [gathered[slot, me, 3 + r] for r in range(3)]
        zero = jnp.zeros_like(x[0])
        rows_of(rows_a, [-2.0 * v for v in x] + [zero] * 3 + [zero + 1.0, dot3(x, x) + core_square])
        rows_of(rows_b, [-v for v in a] + [zero] * 4 + [dot3(a, x)])
        for half, ref in enumerate((rows_a, rows_b)):
            high, middle, low = split3(ref[...].reshape(blocks, SUB, BLOCK))
            pieces = jnp.concatenate([high, middle, low, high, middle, high], 1)
            for b in range(blocks):
                coef[b, half * BLOCK : (half + 1) * BLOCK, :] = pieces[b].T.astype(jnp.bfloat16)

    group = 2 if width % 2 == 0 else 1

    def pair_product(i, j):
        at = [slot_ref[list_ref[i, j + k]] for k in range(group)]
        right = jnp.concatenate([feat[p] for p in at], 1)
        both = lax.dot_general(
            coef[i], right, (((1,), (0,)), ((), ())), preferred_element_type=jnp.float32
        )
        return at, both

    def pair_sums(at, both):
        inverse = lax.rsqrt(both[:BLOCK])
        square = inverse * inverse
        three = square * inverse
        five = three * (square * both[BLOCK:])
        weight = jnp.concatenate([three, five], 0)
        high = weight.astype(jnp.bfloat16)
        low = (weight - high.astype(jnp.float32)).astype(jnp.bfloat16)
        sums = jnp.concatenate([moment[p] for p in at], 1)
        total = 0.0
        for part in (high, low):
            total += lax.dot_general(
                sums, part, (((1,), (1,)), ((), ())), preferred_element_type=jnp.float32
            )
        return total

    def some_targets(first, count):
        work = [(i, j) for i in range(count) for j in range(0, width, group)]
        waiting = []
        totals = [0.0] * count
        for k in range(len(work) + AHEAD):
            if k < len(work):
                i, j = work[k]
                waiting.append((i, pair_product(first + i, j)))
            if k >= AHEAD:
                i, (at, both) = waiting.pop(0)
                totals[i] += pair_sums(at, both)
                if k - AHEAD == len(work) - 1 or work[k - AHEAD + 1][0] != i:
                    whole = totals[i][:SUB] + totals[i][SUB:]
                    at_rows = pl.ds(pl.multiple_of((first + i) * SUB, SUB), SUB)
                    rows_a[at_rows, :] = whole[:, :BLOCK]
                    rows_b[at_rows, :] = whole[:, BLOCK:]

    def all_targets():
        per = TOGETHER if blocks % TOGETHER == 0 else 1

        def body(k, carry):
            some_targets(k * per, per)
            return carry

        lax.fori_loop(0, blocks // per, body, 0)

    def evaluate(slot):
        for d in range(1, spaces):
            copy_to(slot, d).start()
        target_features(slot)
        source_features(slot, me)

        def arrive(d, carry):
            peer, copy = copy_from(slot, d)
            copy.wait_recv()
            source_features(slot, peer)
            return carry

        lax.fori_loop(1, spaces, arrive, 0)
        all_targets()
        x = [gathered[slot, me, r] for r in range(3)]
        a = [gathered[slot, me, 3 + r] for r in range(3)]
        pick = lambda ref, r: ref[pl.ds(r, blocks, stride=SUB), :]
        three_a = [pick(rows_a, r) for r in range(3)]
        three_b = [pick(rows_a, 3 + r) for r in range(3)]
        five_a = [pick(rows_b, r) for r in range(3)]
        five_b = [pick(rows_b, 3 + r) for r in range(3)]
        cross_v = cross(x, three_a)
        cross_s = cross(a, three_a)
        cross_f = cross(x, five_a)
        for r in range(3):
            rate[r] = -inv_four_pi * (cross_v[r] - three_b[r])
            rate[3 + r] = -inv_four_pi * (cross_s[r] - 3.0 * (cross_f[r] - five_b[r]))
        for d in range(1, spaces):
            copy_to(slot, d).wait_send()

    def write_out(value):
        for b in range(blocks):
            for r in range(6):
                out_ref[0, r : r + 1, b * BLOCK : (b + 1) * BLOCK] = value[r, b : b + 1, :]

    second = 3 + g
    steps = jnp.where(g == 0, 4, jnp.where(g < slices - 1, g + 8, g + 7))

    def step(s, carry):
        slot = lax.rem(s, 2)
        other = 1 - slot
        evaluate(slot)
        current = gathered[slot, me]
        now = rate[...]
        part = jnp.where(s < 4, s, s - second)

        @pl.when(part == 0)
        def _():
            base[...] = current
            f0[...] = now
            gathered[other, me] = current + (0.5 * h) * now

        @pl.when(part == 1)
        def _():
            f1[...] = now
            gathered[other, me] = current + (0.5 * h) * now

        @pl.when(part == 2)
        def _():
            f2[...] = now
            gathered[other, me] = base[...] + h * (
                5.0 / 24.0 * f0[...] + 1.0 / 3.0 * f1[...] - 1.0 / 24.0 * now
            )

        @pl.when(part == 3)
        def _():
            end = (
                current
                + (0.5 * h) * (now - f1[...])
                + h * (-1.0 / 24.0 * f0[...] + 1.0 / 3.0 * f1[...] + 5.0 / 24.0 * f2[...])
            )
            coarse = base[...] + h * f0[...]
            correction = end - coarse

            @pl.when(s == 3)
            def _():
                c0[...] = correction

            @pl.when((s > 3) & (g > 1))
            def _():
                pass_copy().wait_recv()
                gathered[other, me] = incoming[...] + correction

            @pl.when((s == 3) | (g <= 1))
            def _():
                gathered[other, me] = coarse + correction

            @pl.when((s > 3) | (g == 0))
            def _():
                write_out(gathered[other, me])

        @pl.when(part < 0)
        def _():
            gathered[other, me] = current + h * now + c0[...]

        @pl.when(part == 4)
        def _():
            outgoing[...] = current + h * now
            copy = pass_copy()
            copy.start()
            copy.wait_send()

        return carry

    lax.fori_loop(0, steps, step, 0)


def per_device(spaces, slices, positions, strengths, source_lists, block_slot):
    blocks, width = source_lists.shape
    whole = block_slot.shape[0]
    state = pltpu.VMEM((6, blocks, BLOCK), jnp.float32)
    vmem = pl.BlockSpec(memory_space=pltpu.VMEM)
    smem = pl.BlockSpec(memory_space=pltpu.SMEM)
    return pl.pallas_call(
        functools.partial(kernel, spaces, slices, blocks, width),
        out_shape=jax.ShapeDtypeStruct((1, 6, blocks * BLOCK), jnp.float32),
        in_specs=[vmem, vmem, smem, smem],
        out_specs=vmem,
        scratch_shapes=[
            pltpu.VMEM((2, spaces, 6, blocks, BLOCK), jnp.float32),
            state, state, state, state, state, state, state, state,
            pltpu.VMEM((blocks * SUB, BLOCK), jnp.float32),
            pltpu.VMEM((blocks * SUB, BLOCK), jnp.float32),
            pltpu.VMEM((whole, PIECES * SUB, BLOCK), jnp.bfloat16),
            pltpu.VMEM((whole, 2 * SUB, BLOCK), jnp.bfloat16),
            pltpu.VMEM((blocks, 2 * BLOCK, PIECES * SUB), jnp.bfloat16),
            pltpu.SemaphoreType.DMA((2, spaces)),
            pltpu.SemaphoreType.DMA((2, spaces)),
            pltpu.SemaphoreType.DMA((2,)),
        ],
        compiler_params=pltpu.CompilerParams(collective_id=0, has_side_effects=True),
    )(positions, strengths, source_lists, block_slot)


def solution(mesh):
    return jax.shard_map(
        functools.partial(per_device, mesh.shape["space"], mesh.shape["tm"]),
        mesh=mesh,
        in_specs=(P(None, "space"), P(None, "space"), P("space", None), P()),
        out_specs=P("tm", None, "space"),
        check_vma=False,
    )
```

```python
import functools

import jax
import jax.numpy as jnp
from jax import lax
from jax.experimental import pallas as pl
from jax.experimental.pallas import tpu as pltpu
from jax.sharding import PartitionSpec as P

BLOCK = 128
SUB = 8
PIECES = 6
TOGETHER = 8
AHEAD = 6
MESH = pl.DeviceIdType.MESH

time_step = 0.1
core_square = 0.25
inv_four_pi = 0.07957747154594767


def cross(u, v):
    return [
        u[1] * v[2] - u[2] * v[1],
        u[2] * v[0] - u[0] * v[2],
        u[0] * v[1] - u[1] * v[0],
    ]


def dot3(u, v):
    return u[0] * v[0] + u[1] * v[1] + u[2] * v[2]


def rounded(v):
    return v.astype(jnp.bfloat16).astype(jnp.float32)


def split3(v):
    high = rounded(v)
    rest = v - high
    middle = rounded(rest)
    return high, middle, rounded(rest - middle)


def kernel(
    spaces, slices, blocks, width,
    pos_ref, str_ref, list_ref, slot_ref, out_ref,
    gathered, base, rate, f0, f1, f2, c0, incoming, outgoing,
    rows_a, rows_b, feat, moment, coef, send_sem, recv_sem, pass_sem,
):
    me = lax.axis_index("space")
    g = lax.axis_index("tm")
    h = time_step

    barrier = pltpu.get_barrier_semaphore()

    def greet(d, carry):
        peer = lax.rem(me + d, spaces)
        pl.semaphore_signal(barrier, inc=1, device_id={"space": peer}, device_id_type=MESH)
        return carry

    lax.fori_loop(1, spaces, greet, 0)

    @pl.when(g > 0)
    def _():
        pl.semaphore_signal(barrier, inc=1, device_id={"tm": g - 1}, device_id_type=MESH)

    @pl.when(g < slices - 1)
    def _():
        pl.semaphore_signal(barrier, inc=1, device_id={"tm": g + 1}, device_id_type=MESH)

    for b in range(blocks):
        cols = slice(b * BLOCK, (b + 1) * BLOCK)
        for r in range(3):
            gathered[0, me, r, b : b + 1, :] = pos_ref[r : r + 1, cols]
            gathered[0, me, 3 + r, b : b + 1, :] = str_ref[r : r + 1, cols]

    neighbours = jnp.where(g > 0, 1, 0) + jnp.where(g < slices - 1, 1, 0)
    pl.semaphore_wait(barrier, spaces - 1 + neighbours)

    chips = spaces // 2
    tall = chips // 2
    core = lax.rem(me, 2)
    column = lax.rem(me // 2, 2)
    row = me // 4
    partner = me + 1 - 2 * core

    def twin(d, sign):
        other_column = lax.rem(column + d % 2, 2)
        other_row = lax.rem(row + tall + sign * (d // 2), tall)
        return 2 * (2 * other_row + other_column) + core

    def copy(slot, what, where, sem):
        return pltpu.make_async_remote_copy(
            src_ref=gathered.at[slot, what],
            dst_ref=gathered.at[slot, what],
            send_sem=send_sem.at[slot, sem],
            recv_sem=recv_sem.at[slot, what],
            device_id={"space": where},
            device_id_type=MESH,
        )

    order = sorted(range(1, chips), key=lambda d: (-(d % 2) - (d // 2), d))

    def mirror(p):
        return p + 1 - 2 * core

    def sends(slot):
        found = [copy(slot, me, twin(d, 1), d) for d in order]
        found += [copy(slot, me, mirror(twin(d, 1)), chips + d) for d in order]
        return found + [copy(slot, me, partner, 0)]

    def pass_copy():
        return pltpu.make_async_remote_copy(
            src_ref=outgoing,
            dst_ref=incoming,
            send_sem=pass_sem.at[0],
            recv_sem=pass_sem.at[1],
            device_id={"tm": lax.rem(g + 1, slices)},
            device_id_type=MESH,
        )

    def rows_of(ref, values):
        for r, v in enumerate(values):
            ref[pl.ds(r, blocks, stride=SUB), :] = v

    def source_features(slot, p):
        x = [gathered[slot, p, r] for r in range(3)]
        a = [gathered[slot, p, 3 + r] for r in range(3)]
        zero = jnp.zeros_like(x[0])
        rows_of(rows_a, x + a + [dot3(x, x), zero + 1.0])
        rows_of(rows_b, a + cross(x, a) + [zero, zero])
        high, middle, low = split3(rows_a[...].reshape(blocks, SUB, BLOCK))
        feat[pl.ds(p * blocks, blocks)] = jnp.concatenate(
            [high, high, high, middle, middle, low], 1
        ).astype(jnp.bfloat16)
        whole = rows_b[...].reshape(blocks, SUB, BLOCK)
        high = rounded(whole)
        moment[pl.ds(p * blocks, blocks)] = jnp.concatenate(
            [high, whole - high], 1
        ).astype(jnp.bfloat16)

    def target_features(slot):
        x = [gathered[slot, me, r] for r in range(3)]
        a = [gathered[slot, me, 3 + r] for r in range(3)]
        zero = jnp.zeros_like(x[0])
        rows_of(rows_a, [-2.0 * v for v in x] + [zero] * 3 + [zero + 1.0, dot3(x, x) + core_square])
        rows_of(rows_b, [-v for v in a] + [zero] * 4 + [dot3(a, x)])
        for half, ref in enumerate((rows_a, rows_b)):
            high, middle, low = split3(ref[...].reshape(blocks, SUB, BLOCK))
            pieces = jnp.concatenate([high, middle, low, high, middle, high], 1)
            for b in range(blocks):
                coef[b, half * BLOCK : (half + 1) * BLOCK, :] = pieces[b].T.astype(jnp.bfloat16)

    group = 2 if width % 2 == 0 else 1

    def pair_product(i, j):
        at = [slot_ref[list_ref[i, j + k]] for k in range(group)]
        right = jnp.concatenate([feat[p] for p in at], 1)
        both = lax.dot_general(
            coef[i], right, (((1,), (0,)), ((), ())), preferred_element_type=jnp.float32
        )
        return at, both

    def pair_sums(at, both):
        inverse = lax.rsqrt(both[:BLOCK])
        square = inverse * inverse
        three = square * inverse
        five = three * (square * both[BLOCK:])
        weight = jnp.concatenate([three, five], 0)
        high = weight.astype(jnp.bfloat16)
        low = (weight - high.astype(jnp.float32)).astype(jnp.bfloat16)
        sums = jnp.concatenate([moment[p] for p in at], 1)
        total = 0.0
        for part in (high, low):
            total += lax.dot_general(
                sums, part, (((1,), (1,)), ((), ())), preferred_element_type=jnp.float32
            )
        return total

    def some_targets(first, count):
        work = [(i, j) for i in range(count) for j in range(0, width, group)]
        waiting = []
        totals = [0.0] * count
        for k in range(len(work) + AHEAD):
            if k < len(work):
                i, j = work[k]
                waiting.append((i, pair_product(first + i, j)))
            if k >= AHEAD:
                i, (at, both) = waiting.pop(0)
                totals[i] += pair_sums(at, both)
                if k - AHEAD == len(work) - 1 or work[k - AHEAD + 1][0] != i:
                    whole = totals[i][:SUB] + totals[i][SUB:]
                    at_rows = pl.ds(pl.multiple_of((first + i) * SUB, SUB), SUB)
                    rows_a[at_rows, :] = whole[:, :BLOCK]
                    rows_b[at_rows, :] = whole[:, BLOCK:]

    def all_targets():
        per = TOGETHER if blocks % TOGETHER == 0 else 1

        def body(k, carry):
            some_targets(k * per, per)
            return carry

        lax.fori_loop(0, blocks // per, body, 0)

    def evaluate(slot):
        for each in sends(slot):
            each.start()
        target_features(slot)
        source_features(slot, me)

        def arrived(p):
            copy(slot, p, p, 0).wait_recv()

        near = order[::-1]
        arrived(partner)
        source_features(slot, partner)
        for d in near:
            arrived(twin(d, -1))
            source_features(slot, twin(d, -1))
        for d in near:
            arrived(mirror(twin(d, -1)))
            source_features(slot, mirror(twin(d, -1)))
        all_targets()
        x = [gathered[slot, me, r] for r in range(3)]
        a = [gathered[slot, me, 3 + r] for r in range(3)]
        pick = lambda ref, r: ref[pl.ds(r, blocks, stride=SUB), :]
        three_a = [pick(rows_a, r) for r in range(3)]
        three_b = [pick(rows_a, 3 + r) for r in range(3)]
        five_a = [pick(rows_b, r) for r in range(3)]
        five_b = [pick(rows_b, 3 + r) for r in range(3)]
        cross_v = cross(x, three_a)
        cross_s = cross(a, three_a)
        cross_f = cross(x, five_a)
        for r in range(3):
            rate[r] = -inv_four_pi * (cross_v[r] - three_b[r])
            rate[3 + r] = -inv_four_pi * (cross_s[r] - 3.0 * (cross_f[r] - five_b[r]))
        for each in sends(slot):
            each.wait_send()

    def write_out(value):
        for b in range(blocks):
            for r in range(6):
                out_ref[0, r : r + 1, b * BLOCK : (b + 1) * BLOCK] = value[r, b : b + 1, :]

    second = 3 + g
    steps = jnp.where(g == 0, 4, jnp.where(g < slices - 1, g + 8, g + 7))

    def step(s, carry):
        slot = lax.rem(s, 2)
        other = 1 - slot
        evaluate(slot)
        current = gathered[slot, me]
        now = rate[...]
        part = jnp.where(s < 4, s, s - second)

        @pl.when(part == 0)
        def _():
            base[...] = current
            f0[...] = now
            gathered[other, me] = current + (0.5 * h) * now

        @pl.when(part == 1)
        def _():
            f1[...] = now
            gathered[other, me] = current + (0.5 * h) * now

        @pl.when(part == 2)
        def _():
            f2[...] = now
            gathered[other, me] = base[...] + h * (
                5.0 / 24.0 * f0[...] + 1.0 / 3.0 * f1[...] - 1.0 / 24.0 * now
            )

        @pl.when(part == 3)
        def _():
            end = (
                current
                + (0.5 * h) * (now - f1[...])
                + h * (-1.0 / 24.0 * f0[...] + 1.0 / 3.0 * f1[...] + 5.0 / 24.0 * f2[...])
            )
            coarse = base[...] + h * f0[...]
            correction = end - coarse

            @pl.when(s == 3)
            def _():
                c0[...] = correction

            @pl.when((s > 3) & (g > 1))
            def _():
                pass_copy().wait_recv()
                gathered[other, me] = incoming[...] + correction

            @pl.when((s == 3) | (g <= 1))
            def _():
                gathered[other, me] = coarse + correction

            @pl.when((s > 3) | (g == 0))
            def _():
                write_out(gathered[other, me])

        @pl.when(part < 0)
        def _():
            gathered[other, me] = current + h * now + c0[...]

        @pl.when(part == 4)
        def _():
            outgoing[...] = current + h * now
            handed = pass_copy()
            handed.start()
            handed.wait_send()

        return carry

    lax.fori_loop(0, steps, step, 0)


def per_device(spaces, slices, positions, strengths, source_lists, block_slot):
    blocks, width = source_lists.shape
    whole = block_slot.shape[0]
    state = pltpu.VMEM((6, blocks, BLOCK), jnp.float32)
    vmem = pl.BlockSpec(memory_space=pltpu.VMEM)
    smem = pl.BlockSpec(memory_space=pltpu.SMEM)
    return pl.pallas_call(
        functools.partial(kernel, spaces, slices, blocks, width),
        out_shape=jax.ShapeDtypeStruct((1, 6, blocks * BLOCK), jnp.float32),
        in_specs=[vmem, vmem, smem, smem],
        out_specs=vmem,
        scratch_shapes=[
            pltpu.VMEM((2, spaces, 6, blocks, BLOCK), jnp.float32),
            state, state, state, state, state, state, state, state,
            pltpu.VMEM((blocks * SUB, BLOCK), jnp.float32),
            pltpu.VMEM((blocks * SUB, BLOCK), jnp.float32),
            pltpu.VMEM((whole, PIECES * SUB, BLOCK), jnp.bfloat16),
            pltpu.VMEM((whole, 2 * SUB, BLOCK), jnp.bfloat16),
            pltpu.VMEM((blocks, 2 * BLOCK, PIECES * SUB), jnp.bfloat16),
            pltpu.SemaphoreType.DMA((2, spaces)),
            pltpu.SemaphoreType.DMA((2, spaces)),
            pltpu.SemaphoreType.DMA((2,)),
        ],
        compiler_params=pltpu.CompilerParams(collective_id=0, has_side_effects=True),
    )(positions, strengths, source_lists, block_slot)


def solution(mesh):
    return jax.shard_map(
        functools.partial(per_device, mesh.shape["space"], mesh.shape["tm"]),
        mesh=mesh,
        in_specs=(P(None, "space"), P(None, "space"), P("space", None), P()),
        out_specs=P("tm", None, "space"),
        check_vma=False,
    )
```
